32 devices in a mesh: groups: 2 (over x), dp: 8 (over z, y), mp: 2 (over core).
Axes of the slice: x: 2, y: 2, z: 4, core: 2. Of those that a mesh axis runs over, the one named last changes fastest.
Arguments:
- residual: bfloat16 [48, 128, 8192], P(('groups', 'dp'), None, 'mp'), parts along dimension 0
- lengths: int32 [48], P(('groups', 'dp')), parts along dimension 0, may hold values from 32 to 128
- labels: int32 [48], P(('groups', 'dp')), parts along dimension 0, may hold values from 0 to 1, as said below
- earlier_means: float32 [16, 79, 2, 8192], P(('groups', 'dp'), None, None, 'mp'), parts along dimension 0
- chosen: int32 [2], P('groups'), parts along dimension 0, may hold values from 0 to 79
- norm_gain: float32 [8192], P('mp'), may hold values from 0.1 to 1.9
- key_weight: bfloat16 [2, 4096, 1024], P('mp', 'dp'), may hold values from -0.0625 to 0.0625
- value_weight: bfloat16 [2, 4096, 1024], P('mp', 'dp'), may hold values from -0.0625 to 0.0625
- out_proj: bfloat16 [2, 8192, 8192], P('groups', 'mp', 'dp'), parts along dimension 0
Outputs:
- directions: float32 [160, 8192], P('groups', 'mp'), parts along dimension 0
- key_cache: bfloat16 [48, 128, 1024], P(('groups', 'dp'), None, 'mp'), parts along dimension 0
- value_cache: bfloat16 [48, 128, 1024], P(('groups', 'dp'), None, 'mp'), parts along dimension 0
- ortho_proj: bfloat16 [2, 8192, 8192], P('groups', 'mp', 'dp'), parts along dimension 0
The draws below stay inside these ranges and needn't reach their ends.
There are 2 independent parts, one for each index of `groups`. The reference program is written for one: setup_inputs(seed, part) draws one part's arguments, and reference() takes and returns one part's arrays. A program takes and returns all parts, laid end to end along the dimension named above; an argument that names none is the same for every part. Nothing has to cross between parts.
Inputs may be any that keep to these rules, and one draw needn't show every extreme that they name: Every slab of 3 consecutive prompts holds both labels.
All inputs are finite; a program needn't handle non-finite values.
Results may differ from the reference program's by a relative error of at most 0.0051.
Values may be sent and summed in bfloat16 or wider, within the bound.
A program may use at most 384 MiB of HBM per device.

```python
import math
import jax
import jax.numpy as jnp
from jax import lax

D = 8192
KV = 1024
LAYERS = 80
LEN = 128
ORTHO = 1
PROMPTS_DEV = 3
PROMPTS = 24
N_DP = 8
N_MP = 2


def feature_scales(key, salt):
    ratio = 6.0
    place = jnp.arange(D, dtype=jnp.float32) / D
    rough = jnp.exp(jax.random.uniform(jax.random.fold_in(key, salt), (D,), jnp.float32, 0.0, math.log(4.0)))
    return jnp.exp(math.log(ratio) * place) * rough


def shared_parts(key):
    slabs = PROMPTS // PROMPTS_DEV
    col_scale = feature_scales(key, 2)
    direction = jax.random.normal(jax.random.fold_in(key, 1), (D,), jnp.float32) * col_scale * 0.25
    slab_counts = jax.random.randint(jax.random.fold_in(key, 3), (slabs, 1), 1, PROMPTS_DEV)
    scores = jax.random.randint(jax.random.fold_in(key, 4), (slabs, PROMPTS_DEV), 0, 1 << 20) * PROMPTS_DEV
    scores = scores + jnp.arange(PROMPTS_DEV, dtype=jnp.int32)[None, :]
    ranks = jnp.argsort(jnp.argsort(scores, axis=1), axis=1)
    label_bits = (ranks < slab_counts).astype(jnp.int32).reshape(PROMPTS)
    return (direction, label_bits)


def draw_labels(key, part):
    return shared_parts(key)[1]


def draw_lengths(key, part):
    base = jax.random.randint(jax.random.fold_in(key, 15), (PROMPTS,), LEN // 4, LEN + 1)
    longest = jax.random.randint(jax.random.fold_in(key, 16), (), 0, PROMPTS)
    shortest = (longest + 1 + jax.random.randint(jax.random.fold_in(key, 17), (), 0, PROMPTS - 1)) % PROMPTS
    index = jnp.arange(PROMPTS, dtype=jnp.int32)
    base = jnp.where(index == longest, LEN, base)
    base = jnp.where(index == shortest, LEN // 4, base)
    return base.astype(jnp.int32)


def draw_residual(key, part):
    direction, label_bits = shared_parts(key)
    signs = (2 * label_bits - 1).astype(jnp.float32)
    strength = jax.random.uniform(jax.random.fold_in(key, 5), (PROMPTS,), jnp.float32, 0.2, 0.6) * signs
    col_noise = feature_scales(key, 7)
    row_scale = jnp.exp(jax.random.uniform(jax.random.fold_in(key, 8), (PROMPTS, LEN, 1), jnp.float32, 0.0, math.log(10.0)))
    noise = jax.random.normal(jax.random.fold_in(key, 6), (PROMPTS, LEN, D), jnp.float32)
    values = (noise * col_noise * 0.3 + strength[:, None, None] * direction[None, None, :]) * row_scale * 0.5
    return values.astype(jnp.bfloat16)


def draw_earlier_means(key, part):
    direction, label_bits = shared_parts(key)
    slabs = PROMPTS // PROMPTS_DEV
    strength = jnp.exp(jax.random.uniform(jax.random.fold_in(key, 10), (LAYERS - 1,), jnp.float32, math.log(0.3), 0.0))
    signs = jnp.array([-1.0, 1.0], jnp.float32)
    col_noise = feature_scales(key, 9)
    noise = 0.5 * jax.random.normal(jax.random.fold_in(key, 11), (slabs, LAYERS - 1, 2, D), jnp.float32)
    noise = noise * col_noise[None, None, None, :]
    return noise + signs[None, None, :, None] * strength[None, :, None, None] * direction[None, None, None, :]


def draw_out_proj(key, part):
    direction, label_bits = shared_parts(key)
    spread = jax.random.normal(jax.random.fold_in(key, 13), (ORTHO, 1, D), jnp.float32)
    noise = jax.random.normal(jax.random.fold_in(key, 14), (ORTHO, D, D), jnp.float32)
    return (noise + 0.2 * direction[None, :, None] * spread).astype(jnp.bfloat16)


def levels(stream_key, shape, pieces, least, top_value):
    def one(position, blocks):
        draws = jax.random.uniform(jax.random.fold_in(jax.random.fold_in(stream_key, 6), position), (blocks,), jnp.float32, least / len(pieces), top_value / len(pieces))
        return jnp.repeat(jnp.exp(draws), shape[position] // blocks).reshape((-1,) + (1,) * (len(shape) - position - 1))

    level = one(*pieces[0])
    for cut in pieces[1:]:
        level = level * one(*cut)
    return level


def scatter_about(stream_key, shape, width, bound, pieces=(), kind=jnp.bfloat16):
    values = jax.random.normal(stream_key, shape, jnp.float32) * width
    if len(pieces) > 0:
        values = levels(stream_key, shape, pieces, -0.22, 0.18) * values
    return jnp.clip(values, min=-bound, max=bound).astype(kind)


def setup_inputs(seed: int = 0, part: int = 0) -> dict:
    streams_of = jax.random.split(jax.random.key(seed), 10)
    part_keys = jax.random.split(jax.random.fold_in(streams_of[9], part), 10)
    return {
        "residual": draw_residual(jax.random.fold_in(jax.random.fold_in(streams_of[9], part), 71), part),
        "lengths": draw_lengths(jax.random.fold_in(jax.random.fold_in(streams_of[9], part), 71), part),
        "labels": draw_labels(jax.random.fold_in(jax.random.fold_in(streams_of[9], part), 71), part),
        "earlier_means": draw_earlier_means(jax.random.fold_in(jax.random.fold_in(streams_of[9], part), 71), part),
        "chosen": jax.random.randint(part_keys[4], (1,), 0, LAYERS).astype(jnp.int32),
        "norm_gain": jnp.clip(1.0 + 0.18 * jax.random.normal(streams_of[5], (D,), jnp.float32), 0.1, 1.9),
        "key_weight": scatter_about(streams_of[6], (N_MP, D // N_MP, KV), D ** -0.5, 0.0625, ((0, 2), (1, 8))),
        "value_weight": scatter_about(streams_of[7], (N_MP, D // N_MP, KV), D ** -0.5, 0.0625, ((0, 2), (1, 8))),
        "out_proj": draw_out_proj(jax.random.fold_in(jax.random.fold_in(streams_of[9], part), 71), part),
    }


def reference(residual, lengths, labels, earlier_means, chosen, norm_gain, key_weight, value_weight, out_proj):
    highest = lax.Precision.HIGHEST
    positions = jnp.arange(LEN, dtype=jnp.int32)
    valid_mask = (positions[None, :] < lengths[:, None]).astype(jnp.float32)
    masked_sums = jnp.einsum('pt,ptd->pd', valid_mask, residual.astype(jnp.float32), precision=highest)
    prompt_mean = masked_sums / lengths.astype(jnp.float32)[:, None]
    onehot = (labels[:, None] == jnp.arange(2, dtype=jnp.int32)[None, :]).astype(jnp.float32)
    onehot = onehot.reshape(N_DP, PROMPTS_DEV, 2)
    counts = lax.optimization_barrier(jnp.sum(onehot, axis=1))
    slab_sums = jnp.einsum('jpc,jpd->jcd', onehot, prompt_mean.reshape(N_DP, PROMPTS_DEV, D), precision=highest)
    current = slab_sums / counts[:, :, None]
    layer_means = jnp.concatenate([earlier_means, current[:, None]], axis=1)
    weighted = jnp.einsum('jc,jlcd->lcd', counts, layer_means, precision=highest)
    merged = weighted / lax.optimization_barrier(jnp.sum(counts, axis=0))[None, :, None]
    difference = merged[:, 1] - merged[:, 0]
    inverse_rms = lax.rsqrt(lax.optimization_barrier(jnp.mean(difference * difference, axis=1)) + 1e-06)
    directions = difference * inverse_rms[:, None]
    refusal_dir = lax.dynamic_index_in_dim(directions, chosen[0], 0, keepdims=False) / math.sqrt(D)
    token_rows = residual.reshape(PROMPTS * LEN, D).astype(jnp.float32)
    projection = jnp.dot(token_rows, refusal_dir, precision=highest)
    ablated = token_rows - projection[:, None] * refusal_dir[None, :]
    mean_square = lax.optimization_barrier(jnp.mean(ablated * ablated, axis=1))
    normed = (ablated * lax.rsqrt(mean_square + 1e-05)[:, None] * norm_gain[None, :]).astype(jnp.bfloat16)
    key_cache = jnp.dot(normed, key_weight.reshape(D, KV), preferred_element_type=jnp.float32)
    value_cache = jnp.dot(normed, value_weight.reshape(D, KV), preferred_element_type=jnp.float32)
    key_cache = key_cache.astype(jnp.bfloat16).reshape(PROMPTS, LEN, KV)
    value_cache = value_cache.astype(jnp.bfloat16).reshape(PROMPTS, LEN, KV)
    matrices = out_proj.astype(jnp.float32)
    column_proj = jnp.einsum('r,ori->oi', refusal_dir, matrices, precision=highest)
    ortho_proj = (matrices - refusal_dir[None, :, None] * column_proj[:, None, :]).astype(jnp.bfloat16)
    return (directions, key_cache, value_cache, ortho_proj)
```

```python
import math

import jax
import jax.numpy as jnp
from jax import lax
from jax.sharding import PartitionSpec as P


def direction_parts(residual, lengths, labels, earlier_means, chosen):
    highest = lax.Precision.HIGHEST
    length = residual.shape[1]
    positions = jnp.arange(length, dtype=jnp.int32)
    valid_mask = (positions[None, :] < lengths[:, None]).astype(jnp.bfloat16)
    masked_sums = jnp.einsum("pt,ptd->pd", valid_mask, residual, preferred_element_type=jnp.float32)
    prompt_mean = masked_sums / lengths.astype(jnp.float32)[:, None]
    onehot = (labels[:, None] == jnp.arange(2, dtype=jnp.int32)[None, :]).astype(jnp.float32)
    counts = jnp.sum(onehot, axis=0)
    current = jnp.sum(onehot[:, :, None] * prompt_mean[:, None, :], axis=0) / counts[:, None]
    earlier = earlier_means[0]
    layers = earlier.shape[0] + 1
    picked = lax.dynamic_index_in_dim(
        earlier, jnp.minimum(chosen[0], layers - 2), 0, keepdims=False
    )
    picked = jnp.where(chosen[0] == layers - 1, current, picked)
    weighted, totals = lax.psum((counts[:, None] * picked, counts), "dp")
    merged = weighted / totals[:, None]
    picked_difference = merged[1] - merged[0]
    share = counts / totals
    local = jnp.concatenate(
        [
            share[1] * earlier[:, 1] - share[0] * earlier[:, 0],
            (share[1] * current[1] - share[0] * current[0])[None],
        ],
        axis=0,
    )
    return picked_difference, local


def shards(
    residual, lengths, labels, earlier_means, chosen, norm_gain, key_weight, value_weight, out_proj
):
    highest = lax.Precision.HIGHEST
    prompts, length, half_width = residual.shape
    model_width = half_width * lax.axis_size("mp")
    picked_difference, local = direction_parts(residual, lengths, labels, earlier_means, chosen)

    key_full = lax.all_gather(key_weight, "dp", axis=1, tiled=True)[0]
    value_full = lax.all_gather(value_weight, "dp", axis=1, tiled=True)[0]

    difference = lax.psum(local, "dp")
    square_sums = lax.psum(jnp.sum(difference * difference, axis=1), "mp")
    directions = difference * lax.rsqrt(square_sums / model_width + 1e-06)[:, None]

    local_square = jnp.sum(picked_difference * picked_difference)
    local_mean = local_square / half_width + 1e-06
    unit = picked_difference * lax.rsqrt(local_mean)
    token_rows = residual.reshape(prompts * length, half_width)
    row_values = token_rows.astype(jnp.float32)
    matrix = out_proj[0]
    dots = jnp.sum(row_values * unit[None, :], axis=1)
    columns = jnp.sum(matrix.astype(jnp.float32) * unit[:, None], axis=0)
    packed = jnp.concatenate([dots, columns, local_square[None]])
    pieces = lax.all_gather(packed, "mp")
    squares = pieces[:, -1]
    mean_dir = jnp.sum(squares) / model_width + 1e-06
    ratios = jnp.sqrt((squares / half_width + 1e-06) / mean_dir) / math.sqrt(model_width)
    sums = jnp.sum(pieces * ratios[:, None], axis=0)
    projection = sums[: prompts * length]
    column_proj = sums[prompts * length : -1]
    refusal_dir = picked_difference * (lax.rsqrt(mean_dir) / math.sqrt(model_width))

    ablated = row_values - projection[:, None] * refusal_dir[None, :]
    mean_square = lax.psum(jnp.sum(ablated * ablated, axis=1), "mp") / model_width
    normed = (ablated * lax.rsqrt(mean_square + 1e-05)[:, None] * norm_gain[None, :]).astype(
        jnp.bfloat16
    )
    ortho_proj = (matrix.astype(jnp.float32) - refusal_dir[:, None] * column_proj[None, :]).astype(
        jnp.bfloat16
    )[None]
    key_sum = jnp.dot(normed, key_full, preferred_element_type=jnp.float32)
    value_sum = jnp.dot(normed, value_full, preferred_element_type=jnp.float32)
    key_sums, value_sums = (
        lax.psum_scatter(key_sum, "mp", scatter_dimension=1, tiled=True),
        lax.psum_scatter(value_sum, "mp", scatter_dimension=1, tiled=True),
    )
    key_cache = key_sums.astype(jnp.bfloat16).reshape(prompts, length, key_sums.shape[1])
    value_cache = value_sums.astype(jnp.bfloat16).reshape(prompts, length, value_sums.shape[1])
    return (directions, key_cache, value_cache, ortho_proj)


def solution(mesh):
    return jax.shard_map(
        shards,
        mesh=mesh,
        in_specs=(
            P(("groups", "dp"), None, "mp"),
            P(("groups", "dp")),
            P(("groups", "dp")),
            P(("groups", "dp"), None, None, "mp"),
            P("groups"),
            P("mp"),
            P("mp", "dp", None),
            P("mp", "dp", None),
            P("groups", "mp", "dp"),
        ),
        out_specs=(
            P("groups", "mp"),
            P(("groups", "dp"), None, "mp"),
            P(("groups", "dp"), None, "mp"),
            P("groups", "mp", "dp"),
        ),
        check_vma=False,
    )
```

```python
import math

import jax
import jax.numpy as jnp
from jax import lax
from jax.sharding import PartitionSpec as P


def direction_parts(residual, lengths, labels, earlier_means, chosen):
    highest = lax.Precision.HIGHEST
    length = residual.shape[1]
    positions = jnp.arange(length, dtype=jnp.int32)
    valid_mask = (positions[None, :] < lengths[:, None]).astype(jnp.bfloat16)
    masked_sums = jnp.einsum("pt,ptd->pd", valid_mask, residual, preferred_element_type=jnp.float32)
    prompt_mean = masked_sums / lengths.astype(jnp.float32)[:, None]
    onehot = (labels[:, None] == jnp.arange(2, dtype=jnp.int32)[None, :]).astype(jnp.float32)
    counts = jnp.sum(onehot, axis=0)
    current = jnp.sum(onehot[:, :, None] * prompt_mean[:, None, :], axis=0) / counts[:, None]
    earlier = earlier_means[0]
    layers = earlier.shape[0] + 1
    picked = lax.dynamic_index_in_dim(
        earlier, jnp.minimum(chosen[0], layers - 2), 0, keepdims=False
    )
    picked = jnp.where(chosen[0] == layers - 1, current, picked)
    weighted, totals = lax.psum((counts[:, None] * picked, counts), "dp")
    merged = weighted / totals[:, None]
    picked_difference = merged[1] - merged[0]
    share = counts / totals
    local = jnp.concatenate(
        [
            share[1] * earlier[:, 1] - share[0] * earlier[:, 0],
            (share[1] * current[1] - share[0] * current[0])[None],
        ],
        axis=0,
    )
    return picked_difference, local


def pair_perm(axis_size):
    return [(i, i ^ 1) for i in range(axis_size)]


def chain_pieces(own, groups, width, parts):
    lines = width // 2
    axes = ("groups", "dp")
    rows = own.shape[0] // parts
    place = lax.axis_index("dp") // 2

    def hop(value, step, way):
        pairs = []
        for g in range(groups):
            for j in range(width):
                z = j // 2
                if way > 0 and step - 1 <= z < lines - 1:
                    pairs.append((g * width + j, g * width + j + 2))
                if way < 0 and 0 < z <= lines - step:
                    pairs.append((g * width + j, g * width + j - 2))
        return lax.ppermute(value, axes, pairs)

    def cross(value, step, way):
        pairs = []
        for g in range(groups):
            for j in range(width):
                z = j // 2
                if (way > 0 and z >= step) or (way < 0 and z < lines - step):
                    pairs.append((g * width + j, (g ^ 1) * width + j))
        return lax.ppermute(value, axes, pairs)

    chain = {}
    crossed = {}
    for way in (1, -1):
        for part in range(parts):
            chain[way, 0, part] = own[part * rows : (part + 1) * rows]
    for step in range(1, lines):
        for part in range(parts):
            for way in (1, -1):
                chain[way, step, part] = hop(chain[way, step - 1, part], step, way)
                crossed[way, step, part] = cross(chain[way, step, part], step, way)

    def merged(table):
        blocks = []
        for step in range(1, lines):
            for part in range(parts):
                blocks.append(
                    jnp.where(place >= step, table[1, step, part], table[-1, lines - step, part])
                )
        return blocks

    return merged(chain), merged(crossed)


def shards(
    residual, lengths, labels, earlier_means, chosen, norm_gain, key_weight, value_weight, out_proj
):
    prompts, length, half_width = residual.shape
    tokens = prompts * length
    model_width = half_width * lax.axis_size("mp")
    groups, width = lax.axis_size("groups"), lax.axis_size("dp")
    lines = width // 2
    block = half_width // width
    even = lax.axis_index("groups") % 2 == 0
    place = lax.axis_index("dp") // 2
    side = lax.axis_index("dp") % 2
    core = lax.axis_index("mp")

    token_rows = residual.reshape(tokens, half_width)
    blocked = token_rows.reshape(tokens, lines, 2 * block)
    wanted = lax.dynamic_slice_in_dim(blocked, (1 - side) * block, block, 2)
    neighbour_rows = lax.ppermute(wanted.reshape(tokens, lines * block), "dp", pair_perm(width))
    key_own, value_own = key_weight[0], value_weight[0]
    chain_own = jnp.where(even, key_own, value_own)
    cross_own = jnp.where(even, value_own, key_own)
    chain, crossed = chain_pieces(chain_own, groups, width, 2)

    picked_difference, local = direction_parts(residual, lengths, labels, earlier_means, chosen)
    difference = lax.psum(local, "dp")
    square_half = jnp.sum(difference * difference, axis=1)
    square_sums = square_half + lax.ppermute(square_half, "mp", pair_perm(2))
    directions = difference * lax.rsqrt(square_sums / model_width + 1e-06)[:, None]

    local_square = jnp.sum(picked_difference * picked_difference)
    local_mean = local_square / half_width + 1e-06
    unit = picked_difference * lax.rsqrt(local_mean)
    row_values = token_rows.astype(jnp.float32)
    matrix = out_proj[0]
    dots = jnp.sum(row_values * unit[None, :], axis=1)
    columns = jnp.sum(matrix.astype(jnp.float32) * unit[:, None], axis=0)
    packed = jnp.concatenate([dots, columns, local_square[None]])
    pieces = lax.all_gather(packed, "mp")
    squares = pieces[:, -1]
    mean_dir = jnp.sum(squares) / model_width + 1e-06
    ratios = jnp.sqrt((squares / half_width + 1e-06) / mean_dir) / math.sqrt(model_width)
    sums = jnp.sum(pieces * ratios[:, None], axis=0)
    projection = sums[:tokens]
    column_proj = sums[tokens:-1]
    refusal_dir = picked_difference * (lax.rsqrt(mean_dir) / math.sqrt(model_width))

    ablated = row_values - projection[:, None] * refusal_dir[None, :]
    mean_square = lax.psum(jnp.sum(ablated * ablated, axis=1), "mp") / model_width
    scale = lax.rsqrt(mean_square + 1e-05)
    ortho_proj = (matrix.astype(jnp.float32) - refusal_dir[:, None] * column_proj[None, :]).astype(
        jnp.bfloat16
    )[None]

    stats = jnp.stack([projection, scale])
    both = jnp.concatenate([stats, lax.ppermute(stats, "dp", pair_perm(width))], axis=1)
    mine = lax.dynamic_slice_in_dim(blocked, side * block, block, 2).reshape(tokens, lines * block)

    def feature_part(vector):
        return lax.dynamic_slice_in_dim(vector.reshape(lines, 2 * block), side * block, block, 1)

    rows = jnp.concatenate([mine, neighbour_rows], axis=0).astype(jnp.float32)
    normed = (
        (rows - both[0][:, None] * feature_part(refusal_dir).reshape(1, -1))
        * both[1][:, None]
        * feature_part(norm_gain).reshape(1, -1)
    ).astype(jnp.bfloat16)
    ordered = jnp.concatenate(
        [
            lax.dynamic_slice_in_dim(normed, (place - step + lines) % lines * block, block, 1)
            for step in range(lines)
        ],
        axis=1,
    )

    def finish(own, blocks):
        weight = jnp.concatenate([own] + blocks, axis=0)
        total = jnp.dot(ordered, weight, preferred_element_type=jnp.float32)
        half = total.shape[1] // 2
        away = lax.dynamic_slice_in_dim(total, (1 - core) * half, half, 1)
        kept = lax.dynamic_slice_in_dim(total, core * half, half, 1)
        kept = kept + lax.ppermute(away, "mp", pair_perm(2))
        result = kept[:tokens] + lax.ppermute(kept[tokens:], "dp", pair_perm(width))
        return result.astype(jnp.bfloat16).reshape(prompts, length, half)

    chain_out = finish(chain_own, chain)
    cross_out = finish(cross_own, crossed)
    key_cache = jnp.where(even, chain_out, cross_out)
    value_cache = jnp.where(even, cross_out, chain_out)
    return (directions, key_cache, value_cache, ortho_proj)


def solution(mesh):
    return jax.shard_map(
        shards,
        mesh=mesh,
        in_specs=(
            P(("groups", "dp"), None, "mp"),
            P(("groups", "dp")),
            P(("groups", "dp")),
            P(("groups", "dp"), None, None, "mp"),
            P("groups"),
            P("mp"),
            P("mp", "dp", None),
            P("mp", "dp", None),
            P("groups", "mp", "dp"),
        ),
        out_specs=(
            P("groups", "mp"),
            P(("groups", "dp"), None, "mp"),
            P(("groups", "dp"), None, "mp"),
            P("groups", "mp", "dp"),
        ),
        check_vma=False,
    )
```

```python
import functools
import math

import jax
import jax.numpy as jnp
from jax import lax
from jax.experimental import pallas as pl
from jax.experimental.pallas import tpu as pltpu
from jax.sharding import PartitionSpec as P

MESH = pl.DeviceIdType.MESH


def direction_parts(residual, lengths, labels, earlier_means, chosen):
    length = residual.shape[1]
    positions = jnp.arange(length, dtype=jnp.int32)
    valid_mask = (positions[None, :] < lengths[:, None]).astype(jnp.bfloat16)
    masked_sums = jnp.einsum("pt,ptd->pd", valid_mask, residual, preferred_element_type=jnp.float32)
    prompt_mean = masked_sums / lengths.astype(jnp.float32)[:, None]
    onehot = (labels[:, None] == jnp.arange(2, dtype=jnp.int32)[None, :]).astype(jnp.float32)
    counts = jnp.sum(onehot, axis=0)
    current = jnp.sum(onehot[:, :, None] * prompt_mean[:, None, :], axis=0) / counts[:, None]
    earlier = earlier_means[0]
    layers = earlier.shape[0] + 1
    picked = lax.dynamic_index_in_dim(
        earlier, jnp.minimum(chosen[0], layers - 2), 0, keepdims=False
    )
    picked = jnp.where(chosen[0] == layers - 1, current, picked)
    packed = jnp.concatenate(
        [
            (counts[:, None] * picked).reshape(-1, 128),
            jnp.broadcast_to(jnp.repeat(counts, 4)[:, None], (8, 128)),
        ],
        axis=0,
    )
    gathered = jnp.sum(gather_small(packed), axis=0)
    totals = gathered[-8::4, 0]
    weighted = gathered[:-8].reshape(2, -1)
    merged = weighted / totals[:, None]
    picked_difference = merged[1] - merged[0]
    share = counts / totals
    local = jnp.concatenate(
        [
            share[1] * earlier[:, 1] - share[0] * earlier[:, 0],
            (share[1] * current[1] - share[0] * current[0])[None],
        ],
        axis=0,
    )
    return picked_difference, local


def pair_perm(axis_size):
    return [(i, i ^ 1) for i in range(axis_size)]


def gather_kernel(peers, mine_ref, all_ref, own_sem, send_sem, recv_sem):
    me = lax.axis_index("dp")
    barrier = pltpu.get_barrier_semaphore()
    for far in range(1, peers):
        pl.semaphore_signal(
            barrier, inc=1, device_id={"dp": lax.rem(me + far, peers)}, device_id_type=MESH
        )
    pl.semaphore_wait(barrier, peers - 1)
    own = pltpu.make_async_copy(mine_ref, all_ref.at[me], own_sem)
    own.start()
    copies = []
    for far in range(1, peers):
        copies.append(
            pltpu.make_async_remote_copy(
                src_ref=mine_ref,
                dst_ref=all_ref.at[me],
                send_sem=send_sem.at[far],
                recv_sem=recv_sem.at[far],
                device_id={"dp": lax.rem(me + far, peers)},
                device_id_type=MESH,
            )
        )
        copies[-1].start()
    own.wait()
    for copy in copies:
        copy.wait_send()
        copy.wait_recv()


def gather_small(value):
    peers = lax.axis_size("dp")
    return pl.pallas_call(
        functools.partial(gather_kernel, peers),
        out_shape=jax.ShapeDtypeStruct((peers,) + value.shape, value.dtype),
        in_specs=[pl.BlockSpec(memory_space=pltpu.VMEM)],
        out_specs=pl.BlockSpec(memory_space=pltpu.VMEM),
        scratch_shapes=[
            pltpu.SemaphoreType.DMA,
            pltpu.SemaphoreType.DMA((peers,)),
            pltpu.SemaphoreType.DMA((peers,)),
        ],
        compiler_params=pltpu.CompilerParams(collective_id=0, has_side_effects=True),
        name="gather_small",
    )(value)


def chain_kernel(
    lines, parts, chain_own, cross_own, wanted, chain_ref, cross_ref, rows_ref, own_sem,
    swap_sem, hop_send, hop_recv, cross_send, cross_recv,
):
    width = 2 * lines
    group, me = lax.axis_index("groups"), lax.axis_index("dp")
    place = me // 2
    beside = me + 1 - 2 * lax.rem(me, 2)
    across = group + 1 - 2 * lax.rem(group, 2)
    rows = chain_own.shape[0] // parts
    barrier = pltpu.get_barrier_semaphore()

    for far in range(1, width):
        pl.semaphore_signal(
            barrier, inc=1, device_id={"dp": lax.rem(me + far, width)}, device_id_type=MESH
        )
    pl.semaphore_signal(barrier, inc=1, device_id={"groups": across}, device_id_type=MESH)
    pl.semaphore_wait(barrier, width)

    def hop(step, part, way):
        k = 0 if way > 0 else 1
        slot = lax.rem(place - way * (step - 1) + lines, lines)
        here = pl.ds(part * rows, rows)
        source = chain_own.at[here] if step == 1 else chain_ref.at[slot, here]
        return pltpu.make_async_remote_copy(
            src_ref=source,
            dst_ref=chain_ref.at[slot, here],
            send_sem=hop_send.at[k, step, part],
            recv_sem=hop_recv.at[k, step, part],
            device_id={"dp": lax.rem(me + 2 * way + width, width)},
            device_id_type=MESH,
        )

    def arrival(step, part, way):
        k = 0 if way > 0 else 1
        slot = lax.rem(place - way * step + lines, lines)
        here = pl.ds(part * rows, rows)
        landed = chain_ref.at[slot, here]
        return pltpu.make_async_remote_copy(
            src_ref=landed,
            dst_ref=landed,
            send_sem=hop_send.at[k, step, part],
            recv_sem=hop_recv.at[k, step, part],
            device_id={"dp": lax.rem(me - 2 * way + width, width)},
            device_id_type=MESH,
        )

    def cross(step, part, way):
        k = 0 if way > 0 else 1
        slot = lax.rem(place - way * step + lines, lines)
        here = pl.ds(part * rows, rows)
        return pltpu.make_async_remote_copy(
            src_ref=chain_ref.at[slot, here],
            dst_ref=cross_ref.at[slot, here],
            send_sem=cross_send.at[k, step, part],
            recv_sem=cross_recv.at[k, step, part],
            device_id={"groups": across},
            device_id_type=MESH,
        )

    def sends(step, way):
        return (place >= step - 1) & (place < lines - 1) if way > 0 else (
            (place > 0) & (place <= lines - step)
        )

    def holds(step, way):
        return place >= step if way > 0 else place < lines - step

    for part in range(parts):
        for way in (1, -1):

            @pl.when(sends(1, way))
            def _():
                hop(1, part, way).start()

    swap = pltpu.make_async_remote_copy(
        src_ref=wanted,
        dst_ref=rows_ref,
        send_sem=swap_sem.at[0],
        recv_sem=swap_sem.at[1],
        device_id={"dp": beside},
        device_id_type=MESH,
    )
    swap.start()
    keep_chain = pltpu.make_async_copy(chain_own, chain_ref.at[place], own_sem.at[0])
    keep_cross = pltpu.make_async_copy(cross_own, cross_ref.at[place], own_sem.at[1])
    keep_chain.start()
    keep_cross.start()

    for step in range(1, lines):
        for part in range(parts):
            for way in (1, -1):

                @pl.when(holds(step, way))
                def _():
                    arrival(step, part, way).wait_recv()
                    if step < lines - 1:

                        @pl.when(sends(step + 1, way))
                        def _():
                            hop(step + 1, part, way).start()

                    cross(step, part, way).start()

    keep_chain.wait()
    keep_cross.wait()
    swap.wait_send()
    swap.wait_recv()
    for step in range(1, lines):
        for part in range(parts):
            for way in (1, -1):

                @pl.when(sends(step, way))
                def _():
                    hop(step, part, way).wait_send()

                @pl.when(holds(step, way))
                def _():
                    cross(step, part, way).wait_send()
                    cross(step, part, way).wait_recv()


def chain_gather(chain_own, cross_own, wanted, lines, parts):
    full = jax.ShapeDtypeStruct((lines,) + chain_own.shape, chain_own.dtype)
    any_spec = pl.BlockSpec(memory_space=pl.ANY)
    return pl.pallas_call(
        functools.partial(chain_kernel, lines, parts),
        out_shape=(full, full, jax.ShapeDtypeStruct(wanted.shape, wanted.dtype)),
        in_specs=[any_spec] * 3,
        out_specs=[any_spec] * 3,
        scratch_shapes=[
            pltpu.SemaphoreType.DMA((2,)),
            pltpu.SemaphoreType.DMA((2,)),
        ]
        + [pltpu.SemaphoreType.DMA((2, lines, parts))] * 4,
        compiler_params=pltpu.CompilerParams(collective_id=1, has_side_effects=True),
        cost_estimate=pl.CostEstimate(flops=0, transcendentals=0, bytes_accessed=200 << 20),
        name="chain_gather",
    )(chain_own, cross_own, wanted)


def shards(
    residual, lengths, labels, earlier_means, chosen, norm_gain, key_weight, value_weight, out_proj
):
    prompts, length, half_width = residual.shape
    tokens = prompts * length
    model_width = half_width * lax.axis_size("mp")
    groups, width = lax.axis_size("groups"), lax.axis_size("dp")
    lines = width // 2
    block = half_width // width
    even = lax.axis_index("groups") % 2 == 0
    side = lax.axis_index("dp") % 2
    core = lax.axis_index("mp")

    token_rows = residual.reshape(tokens, half_width)
    blocked = token_rows.reshape(tokens, lines, 2 * block)
    wanted = lax.dynamic_slice_in_dim(blocked, (1 - side) * block, block, 2)
    key_own, value_own = key_weight[0], value_weight[0]
    chain_own = jnp.where(even, key_own, value_own)
    cross_own = jnp.where(even, value_own, key_own)
    picked_difference, local = direction_parts(residual, lengths, labels, earlier_means, chosen)
    local, wanted = lax.optimization_barrier((local, wanted.reshape(tokens, lines * block)))
    difference = lax.psum(local, "dp")
    chain, crossed, neighbour_rows = chain_gather(chain_own, cross_own, wanted, lines, 4)

    local_square = jnp.sum(picked_difference * picked_difference)
    local_mean = local_square / half_width + 1e-06
    unit = picked_difference * lax.rsqrt(local_mean)
    row_values = token_rows.astype(jnp.float32)
    matrix = out_proj[0]
    dots = jnp.sum(row_values * unit[None, :], axis=1)
    columns = jnp.sum(matrix.astype(jnp.float32) * unit[:, None], axis=0)
    packed = jnp.concatenate([dots, columns, local_square[None]])
    pieces = lax.all_gather(packed, "mp")
    squares = pieces[:, -1]
    mean_dir = jnp.sum(squares) / model_width + 1e-06
    ratios = jnp.sqrt((squares / half_width + 1e-06) / mean_dir) / math.sqrt(model_width)
    sums = jnp.sum(pieces * ratios[:, None], axis=0)
    projection = sums[:tokens]
    column_proj = sums[tokens:-1]
    refusal_dir = picked_difference * (lax.rsqrt(mean_dir) / math.sqrt(model_width))

    ablated = row_values - projection[:, None] * refusal_dir[None, :]
    mean_square = lax.psum(jnp.sum(ablated * ablated, axis=1), "mp") / model_width
    scale = lax.rsqrt(mean_square + 1e-05)
    ortho_proj = (matrix.astype(jnp.float32) - refusal_dir[:, None] * column_proj[None, :]).astype(
        jnp.bfloat16
    )[None]

    stats = jnp.stack([projection, scale])
    both = jnp.concatenate([stats, lax.ppermute(stats, "dp", pair_perm(width))], axis=1)
    mine = lax.dynamic_slice_in_dim(blocked, side * block, block, 2).reshape(tokens, lines * block)

    def feature_part(vector):
        return lax.dynamic_slice_in_dim(vector.reshape(lines, 2 * block), side * block, block, 1)

    rows = jnp.concatenate([mine, neighbour_rows], axis=0).astype(jnp.float32)
    normed = (
        (rows - both[0][:, None] * feature_part(refusal_dir).reshape(1, -1))
        * both[1][:, None]
        * feature_part(norm_gain).reshape(1, -1)
    ).astype(jnp.bfloat16)
    def finish(weight):
        weight = weight.reshape(lines * block, -1)
        total = jnp.dot(normed, weight, preferred_element_type=jnp.float32)
        half = total.shape[1] // 2
        away = lax.dynamic_slice_in_dim(total, (1 - core) * half, half, 1)
        kept = lax.dynamic_slice_in_dim(total, core * half, half, 1)
        kept = kept + lax.ppermute(away, "mp", pair_perm(2))
        result = kept[:tokens] + lax.ppermute(kept[tokens:], "dp", pair_perm(width))
        return result.astype(jnp.bfloat16).reshape(prompts, length, half)

    chain_out = finish(chain)
    cross_out = finish(crossed)
    difference, normed = lax.optimization_barrier((difference, normed))
    square_half = jnp.sum(difference * difference, axis=1)
    square_sums = square_half + lax.ppermute(square_half, "mp", pair_perm(2))
    directions = difference * lax.rsqrt(square_sums / model_width + 1e-06)[:, None]

    key_cache = jnp.where(even, chain_out, cross_out)
    value_cache = jnp.where(even, cross_out, chain_out)
    return (directions, key_cache, value_cache, ortho_proj)


def solution(mesh):
    return jax.shard_map(
        shards,
        mesh=mesh,
        in_specs=(
            P(("groups", "dp"), None, "mp"),
            P(("groups", "dp")),
            P(("groups", "dp")),
            P(("groups", "dp"), None, None, "mp"),
            P("groups"),
            P("mp"),
            P("mp", "dp", None),
            P("mp", "dp", None),
            P("groups", "mp", "dp"),
        ),
        out_specs=(
            P("groups", "mp"),
            P(("groups", "dp"), None, "mp"),
            P(("groups", "dp"), None, "mp"),
            P("groups", "mp", "dp"),
        ),
        check_vma=False,
    )
```

```python
import functools
import math

import jax
import jax.numpy as jnp
from jax import lax
from jax.experimental import pallas as pl
from jax.experimental.pallas import tpu as pltpu
from jax.sharding import PartitionSpec as P

MESH = pl.DeviceIdType.MESH


def direction_parts(residual, lengths, labels, earlier_means, chosen):
    length = residual.shape[1]
    positions = jnp.arange(length, dtype=jnp.int32)
    valid_mask = (positions[None, :] < lengths[:, None]).astype(jnp.bfloat16)
    masked_sums = jnp.einsum("pt,ptd->pd", valid_mask, residual, preferred_element_type=jnp.float32)
    prompt_mean = masked_sums / lengths.astype(jnp.float32)[:, None]
    onehot = (labels[:, None] == jnp.arange(2, dtype=jnp.int32)[None, :]).astype(jnp.float32)
    counts = jnp.sum(onehot, axis=0)
    current = jnp.sum(onehot[:, :, None] * prompt_mean[:, None, :], axis=0) / counts[:, None]
    earlier = earlier_means[0]
    layers = earlier.shape[0] + 1
    picked = lax.dynamic_index_in_dim(
        earlier, jnp.minimum(chosen[0], layers - 2), 0, keepdims=False
    )
    picked = jnp.where(chosen[0] == layers - 1, current, picked)
    packed = jnp.concatenate(
        [
            (counts[:, None] * picked).reshape(-1, 128),
            jnp.broadcast_to(jnp.repeat(counts, 4)[:, None], (8, 128)),
        ],
        axis=0,
    )
    gathered = jnp.sum(gather_small(packed), axis=0)
    totals = gathered[-8::4, 0]
    weighted = gathered[:-8].reshape(2, -1)
    merged = weighted / totals[:, None]
    picked_difference = merged[1] - merged[0]
    share = counts / totals
    local = jnp.concatenate(
        [
            share[1] * earlier[:, 1] - share[0] * earlier[:, 0],
            (share[1] * current[1] - share[0] * current[0])[None],
        ],
        axis=0,
    )
    return picked_difference, local


def pair_perm(axis_size):
    return [(i, i ^ 1) for i in range(axis_size)]


def gather_kernel(peers, mine_ref, all_ref, own_sem, send_sem, recv_sem):
    me = lax.axis_index("dp")
    barrier = pltpu.get_barrier_semaphore()
    for far in range(1, peers):
        pl.semaphore_signal(
            barrier, inc=1, device_id={"dp": lax.rem(me + far, peers)}, device_id_type=MESH
        )
    pl.semaphore_wait(barrier, peers - 1)
    own = pltpu.make_async_copy(mine_ref, all_ref.at[me], own_sem)
    own.start()
    copies = []
    for far in range(1, peers):
        copies.append(
            pltpu.make_async_remote_copy(
                src_ref=mine_ref,
                dst_ref=all_ref.at[me],
                send_sem=send_sem.at[far],
                recv_sem=recv_sem.at[far],
                device_id={"dp": lax.rem(me + far, peers)},
                device_id_type=MESH,
            )
        )
        copies[-1].start()
    own.wait()
    for copy in copies:
        copy.wait_send()
        copy.wait_recv()


def gather_small(value):
    peers = lax.axis_size("dp")
    return pl.pallas_call(
        functools.partial(gather_kernel, peers),
        out_shape=jax.ShapeDtypeStruct((peers,) + value.shape, value.dtype),
        in_specs=[pl.BlockSpec(memory_space=pltpu.VMEM)],
        out_specs=pl.BlockSpec(memory_space=pltpu.VMEM),
        scratch_shapes=[
            pltpu.SemaphoreType.DMA,
            pltpu.SemaphoreType.DMA((peers,)),
            pltpu.SemaphoreType.DMA((peers,)),
        ],
        compiler_params=pltpu.CompilerParams(collective_id=0, has_side_effects=True),
        name="gather_small",
    )(value)


def chain_kernel(
    lines, parts, chain_own, cross_own, wanted, chain_ref, cross_ref, rows_ref, own_sem,
    swap_sem, hop_send, hop_recv, cross_send, cross_recv,
):
    width = 2 * lines
    group, me = lax.axis_index("groups"), lax.axis_index("dp")
    place = me // 2
    beside = me + 1 - 2 * lax.rem(me, 2)
    across = group + 1 - 2 * lax.rem(group, 2)
    rows = chain_own.shape[0] // parts
    barrier = pltpu.get_barrier_semaphore()

    for far in range(1, width):
        pl.semaphore_signal(
            barrier, inc=1, device_id={"dp": lax.rem(me + far, width)}, device_id_type=MESH
        )
    pl.semaphore_signal(barrier, inc=1, device_id={"groups": across}, device_id_type=MESH)
    pl.semaphore_wait(barrier, width)

    def hop(step, part, way):
        k = 0 if way > 0 else 1
        slot = lax.rem(place - way * (step - 1) + lines, lines)
        here = pl.ds(part * rows, rows)
        source = chain_own.at[here] if step == 1 else chain_ref.at[slot, here]
        return pltpu.make_async_remote_copy(
            src_ref=source,
            dst_ref=chain_ref.at[slot, here],
            send_sem=hop_send.at[k, step, part],
            recv_sem=hop_recv.at[k, step, part],
            device_id={"dp": lax.rem(me + 2 * way + width, width)},
            device_id_type=MESH,
        )

    def arrival(step, part, way):
        k = 0 if way > 0 else 1
        slot = lax.rem(place - way * step + lines, lines)
        here = pl.ds(part * rows, rows)
        landed = chain_ref.at[slot, here]
        return pltpu.make_async_remote_copy(
            src_ref=landed,
            dst_ref=landed,
            send_sem=hop_send.at[k, step, part],
            recv_sem=hop_recv.at[k, step, part],
            device_id={"dp": lax.rem(me - 2 * way + width, width)},
            device_id_type=MESH,
        )

    def cross(step, part, way):
        k = 0 if way > 0 else 1
        slot = lax.rem(place - way * step + lines, lines)
        here = pl.ds(part * rows, rows)
        return pltpu.make_async_remote_copy(
            src_ref=chain_ref.at[slot, here],
            dst_ref=cross_ref.at[slot, here],
            send_sem=cross_send.at[k, step, part],
            recv_sem=cross_recv.at[k, step, part],
            device_id={"groups": across},
            device_id_type=MESH,
        )

    def sends(step, way):
        return (place >= step - 1) & (place < lines - 1) if way > 0 else (
            (place > 0) & (place <= lines - step)
        )

    def holds(step, way):
        return place >= step if way > 0 else place < lines - step

    for part in range(parts):
        for way in (1, -1):

            @pl.when(sends(1, way))
            def _():
                hop(1, part, way).start()

    swap = pltpu.make_async_remote_copy(
        src_ref=wanted,
        dst_ref=rows_ref,
        send_sem=swap_sem.at[0],
        recv_sem=swap_sem.at[1],
        device_id={"dp": beside},
        device_id_type=MESH,
    )
    swap.start()
    keep_chain = pltpu.make_async_copy(chain_own, chain_ref.at[place], own_sem.at[0])
    keep_cross = pltpu.make_async_copy(cross_own, cross_ref.at[place], own_sem.at[1])
    keep_chain.start()
    keep_cross.start()

    for step in range(1, lines):
        for part in range(parts):
            for way in (1, -1):

                @pl.when(holds(step, way))
                def _():
                    arrival(step, part, way).wait_recv()
                    if step < lines - 1:

                        @pl.when(sends(step + 1, way))
                        def _():
                            hop(step + 1, part, way).start()

                    cross(step, part, way).start()

    keep_chain.wait()
    keep_cross.wait()
    swap.wait_send()
    swap.wait_recv()
    for step in range(1, lines):
        for part in range(parts):
            for way in (1, -1):

                @pl.when(sends(step, way))
                def _():
                    hop(step, part, way).wait_send()

                @pl.when(holds(step, way))
                def _():
                    cross(step, part, way).wait_send()
                    cross(step, part, way).wait_recv()


def chain_gather(chain_own, cross_own, wanted, lines, parts):
    full = jax.ShapeDtypeStruct((lines,) + chain_own.shape, chain_own.dtype)
    any_spec = pl.BlockSpec(memory_space=pl.ANY)
    return pl.pallas_call(
        functools.partial(chain_kernel, lines, parts),
        out_shape=(full, full, jax.ShapeDtypeStruct(wanted.shape, wanted.dtype)),
        in_specs=[any_spec] * 3,
        out_specs=[any_spec] * 3,
        scratch_shapes=[
            pltpu.SemaphoreType.DMA((2,)),
            pltpu.SemaphoreType.DMA((2,)),
        ]
        + [pltpu.SemaphoreType.DMA((2, lines, parts))] * 4,
        compiler_params=pltpu.CompilerParams(collective_id=1, has_side_effects=True),
        cost_estimate=pl.CostEstimate(flops=0, transcendentals=0, bytes_accessed=200 << 20),
        name="chain_gather",
    )(chain_own, cross_own, wanted)


def shards(
    residual, lengths, labels, earlier_means, chosen, norm_gain, key_weight, value_weight, out_proj
):
    prompts, length, half_width = residual.shape
    tokens = prompts * length
    model_width = half_width * lax.axis_size("mp")
    groups, width = lax.axis_size("groups"), lax.axis_size("dp")
    lines = width // 2
    block = half_width // width
    even = lax.axis_index("groups") % 2 == 0
    side = lax.axis_index("dp") % 2
    core = lax.axis_index("mp")

    token_rows = residual.reshape(tokens, half_width)
    blocked = token_rows.reshape(tokens, lines, 2 * block)
    wanted = lax.dynamic_slice_in_dim(blocked, (1 - side) * block, block, 2)
    key_own, value_own = key_weight[0], value_weight[0]
    chain_own = jnp.where(even, key_own, value_own)
    cross_own = jnp.where(even, value_own, key_own)
    picked_difference, local = direction_parts(residual, lengths, labels, earlier_means, chosen)
    local, wanted = lax.optimization_barrier((local, wanted.reshape(tokens, lines * block)))
    difference = lax.psum(local, "dp")
    chain, crossed, neighbour_rows = chain_gather(chain_own, cross_own, wanted, lines, 8)

    local_square = jnp.sum(picked_difference * picked_difference)
    local_mean = local_square / half_width + 1e-06
    unit = picked_difference * lax.rsqrt(local_mean)
    row_values = token_rows.astype(jnp.float32)
    matrix = out_proj[0]
    dots = jnp.sum(row_values * unit[None, :], axis=1)
    packed = jnp.concatenate([dots, local_square[None]])
    pieces = lax.all_gather(packed, "mp")
    squares = pieces[:, -1]
    mean_dir = jnp.sum(squares) / model_width + 1e-06
    ratios = jnp.sqrt((squares / half_width + 1e-06) / mean_dir) / math.sqrt(model_width)
    sums = jnp.sum(pieces * ratios[:, None], axis=0)
    projection = sums[:tokens]
    refusal_dir = picked_difference * (lax.rsqrt(mean_dir) / math.sqrt(model_width))

    ablated = row_values - projection[:, None] * refusal_dir[None, :]
    mean_square = lax.psum(jnp.sum(ablated * ablated, axis=1), "mp") / model_width
    scale = lax.rsqrt(mean_square + 1e-05)
    stats = jnp.stack([projection, scale])
    both = jnp.concatenate([stats, lax.ppermute(stats, "dp", pair_perm(width))], axis=1)
    mine = lax.dynamic_slice_in_dim(blocked, side * block, block, 2).reshape(tokens, lines * block)

    def feature_part(vector):
        return lax.dynamic_slice_in_dim(vector.reshape(lines, 2 * block), side * block, block, 1)

    rows = jnp.concatenate([mine, neighbour_rows], axis=0).astype(jnp.float32)
    normed = (
        (rows - both[0][:, None] * feature_part(refusal_dir).reshape(1, -1))
        * both[1][:, None]
        * feature_part(norm_gain).reshape(1, -1)
    ).astype(jnp.bfloat16)
    matrix, normed = lax.optimization_barrier((matrix, normed))
    columns = jnp.sum(matrix.astype(jnp.float32) * unit[:, None], axis=0)
    swapped = lax.ppermute(columns, "mp", pair_perm(2))
    column_proj = columns * ratios[core] + swapped * ratios[1 - core]
    ortho_proj = (matrix.astype(jnp.float32) - refusal_dir[:, None] * column_proj[None, :]).astype(
        jnp.bfloat16
    )[None]

    def finish(weight):
        weight = weight.reshape(lines * block, -1)
        total = jnp.dot(normed, weight, preferred_element_type=jnp.float32)
        half = total.shape[1] // 2
        away = lax.dynamic_slice_in_dim(total, (1 - core) * half, half, 1)
        kept = lax.dynamic_slice_in_dim(total, core * half, half, 1)
        kept = kept + lax.ppermute(away, "mp", pair_perm(2))
        result = kept[:tokens] + lax.ppermute(kept[tokens:], "dp", pair_perm(width))
        return result.astype(jnp.bfloat16).reshape(prompts, length, half)

    chain_out = finish(chain)
    cross_out = finish(crossed)
    difference, normed = lax.optimization_barrier((difference, normed))
    square_half = jnp.sum(difference * difference, axis=1)
    square_sums = square_half + lax.ppermute(square_half, "mp", pair_perm(2))
    directions = difference * lax.rsqrt(square_sums / model_width + 1e-06)[:, None]

    key_cache = jnp.where(even, chain_out, cross_out)
    value_cache = jnp.where(even, cross_out, chain_out)
    return (directions, key_cache, value_cache, ortho_proj)


def solution(mesh):
    return jax.shard_map(
        shards,
        mesh=mesh,
        in_specs=(
            P(("groups", "dp"), None, "mp"),
            P(("groups", "dp")),
            P(("groups", "dp")),
            P(("groups", "dp"), None, None, "mp"),
            P("groups"),
            P("mp"),
            P("mp", "dp", None),
            P("mp", "dp", None),
            P("groups", "mp", "dp"),
        ),
        out_specs=(
            P("groups", "mp"),
            P(("groups", "dp"), None, "mp"),
            P(("groups", "dp"), None, "mp"),
            P("groups", "mp", "dp"),
        ),
        check_vma=False,
    )
```
